32 devices in a mesh: tm: 8 (over y, x, core), space: 4 (over z).
Axes of the slice: x: 2, y: 2, z: 4, core: 2. Of those that a mesh axis runs over, the one named last changes fastest.
Arguments:
- steps: bfloat16 [24, 1024, 1024], P('tm', 'space'), as said below
- lengths: int32 [8], P('tm'), may hold values from 1 to 3, 16 in all
- anchor: bfloat16 [1024, 2048], P(None, 'space'), may hold values from -6 to 6
Outputs:
- panels: float32 [24, 1024, 2048], P('tm', None, 'space')
The draws below stay inside these ranges and needn't reach their ends.
Inputs may be any that keep to these rules, and one draw needn't show every extreme that they name: `steps`: slots of a section beyond its length hold entries that no output reads.
All inputs are finite; a program needn't handle non-finite values. No bound on the sum of `lengths` on one device may be relied on, other than what follows from the above.
Results may differ from the reference program's by a relative error of at most 0.025.
Values may be sent and summed in bfloat16 or wider, within the bound.
A program may use at most 64 MiB of HBM per device.

```python
import math
import jax
import jax.numpy as jnp
import numpy as np
from jax import lax

MESH_NODES = 1024
CAP = 3
COLS = 2048
DAY_SLOTS = 24
N_TM = 8


def draw_steps(key, part):
    intensity_key, noise_random_key, displacement_key, spike_random_key, selection_key = jax.random.split(jax.random.fold_in(key, 11), 5)
    rate_low = 0.004
    rate_high = 0.4
    spread = math.log(rate_high / rate_low)
    mean_inverse = 1.03 * (1.0 / rate_low - 1.0 / rate_high) / (2.0 * spread) + 0.5 + (rate_high - rate_low) / (6.0 * spread)
    coupling_scale = 1.0 / math.sqrt(mean_inverse)
    channel_rates = jnp.exp(jax.random.uniform(intensity_key, (1, MESH_NODES), jnp.float32, math.log(rate_low), math.log(rate_high)))
    jitter = jnp.exp(jax.random.uniform(noise_random_key, (DAY_SLOTS, MESH_NODES), jnp.float32, math.log(0.7), math.log(1.4)))
    spike_slot_list = jax.random.uniform(spike_random_key, (DAY_SLOTS, 1), jnp.float32) < 0.08
    spike_channel_list = jax.random.uniform(selection_key, (DAY_SLOTS, MESH_NODES), jnp.float32) < 0.25
    spike_layout = jnp.where(spike_slot_list & spike_channel_list, 0.6, 1.0)
    diagonal_entries = jnp.exp(-channel_rates * jitter) * spike_layout
    coupling = jax.random.normal(displacement_key, (DAY_SLOTS, MESH_NODES, MESH_NODES), jnp.float32) * (coupling_scale / math.sqrt(MESH_NODES))
    identity = jnp.eye(MESH_NODES, dtype=jnp.float32)
    return (coupling + diagonal_entries[:, :, None] * identity[None]).astype(jnp.bfloat16)


def block_levels(own_key, shape, cuts, least, largest):
    loudness = 1.0
    for dim, parts in cuts:
        draws = jax.random.uniform(jax.random.fold_in(jax.random.fold_in(own_key, 6), dim), (parts,), jnp.float32, least / len(cuts), largest / len(cuts))
        loudness = loudness * jnp.repeat(jnp.exp(draws), shape[dim] // parts).reshape((-1,) + (1,) * (len(shape) - 1 - dim))
    return loudness


def length_profile(count, total, reach, slope):
    loads = [(1 << 20) // math.isqrt(standing ** slope) + 1 for standing in range(2, count + 1)]
    rest, counts = total - reach - (count - 1), [1] * (count - 1)
    while rest > 0:
        free = [i for i in range(count - 1) if counts[i] < reach]
        pool, budget = sum([loads[i] for i in free]), rest
        for i in free:
            addition = min(reach - counts[i], max(1, budget * loads[i] // pool), rest)
            counts[i] = counts[i] + addition
            rest = rest - addition
    return np.array([reach] + counts)


def ragged(key, number_of, total, limit, slope):
    if number_of == 2:
        one = jax.random.randint(key, (), max(1, total - limit), min(limit, total - 1) + 1)
        return jnp.stack([one, total - one])
    sizes = jnp.asarray(length_profile(number_of, total, limit, slope), jnp.int32)
    pairs = (number_of - 1) // 2
    donor, receiver = sizes[1:1 + 2 * pairs:2], sizes[2:2 + 2 * pairs:2]
    room = jnp.minimum(donor - 1, limit - receiver)
    shifted = jax.random.randint(jax.random.fold_in(key, 1), (pairs,), 0, 1 << 20) % (room + 1)
    sizes = sizes.at[1:1 + 2 * pairs:2].set(donor - shifted).at[2:2 + 2 * pairs:2].set(receiver + shifted)
    return sizes[jax.random.permutation(jax.random.fold_in(key, 2), number_of)]


def bell_draw(own_key, dims, width, limit, cuts=(), held_as=jnp.bfloat16):
    level = block_levels(own_key, dims, cuts, -0.22, 0.18) if cuts else 1.0
    array = jax.random.normal(own_key, dims, jnp.float32) * width * level
    return jnp.minimum(jnp.maximum(array, -limit), limit).astype(held_as)


def setup_inputs(seed: int = 0) -> dict:
    arg_keys = jax.random.split(jax.random.key(seed), 4)
    return {
        "steps": draw_steps(jax.random.fold_in(arg_keys[3], 71), 0),
        "lengths": ragged(arg_keys[1], N_TM, 2 * N_TM, CAP, 2).astype(jnp.int32),
        "anchor": bell_draw(arg_keys[2], (MESH_NODES, COLS), 1.0, 6.0, ((1, 4),)),
    }


def reference(steps, lengths, anchor):
    slots_all = jnp.arange(DAY_SLOTS - 1, -1, -1).astype(jnp.int32)

    def advance(carry, slot):
        section = slot // CAP
        within = slot % CAP
        used = within < lengths[section]
        result = lax.cond(used, lambda: jnp.dot(steps[slot], carry, preferred_element_type=jnp.float32), lambda: jnp.zeros((MESH_NODES, COLS), jnp.float32))
        carry = jnp.where(used, result.astype(jnp.bfloat16), carry)
        return carry, result

    final, results = lax.scan(advance, anchor, slots_all)
    return results[::-1]
```

```python
import functools

import jax
import jax.numpy as jnp
from jax import lax
from jax.experimental import pallas as pl
from jax.experimental.pallas import tpu as pltpu
from jax.sharding import PartitionSpec as P

MESH = pl.DeviceIdType.MESH
CHUNK = 128
TILE = 256


def kernel(
    nt, nz, len_ref, steps_ref, anchor_ref, out_ref, full, carry, gsend, grecv, csend, crecv
):
    t, z = lax.axis_index("tm"), lax.axis_index("space")
    cap, rows, nodes = steps_ref.shape
    width = anchor_ref.shape[1]
    chunk = min(CHUNK, width)
    tile = min(TILE, nodes)

    barrier = pltpu.get_barrier_semaphore()
    for axis, at, size in (("tm", t, nt), ("space", z, nz)):
        for step in (1, size - 1):
            pl.semaphore_signal(
                barrier,
                inc=1,
                device_id={axis: lax.rem(at + step, size)},
                device_id_type=MESH,
            )
    pl.semaphore_wait(barrier, 4)

    def place(slot, owner):
        return full.at[slot, pl.ds(pl.multiple_of(owner * rows, rows), rows)]

    def hop(slot, s, way):
        owner = z - way * s
        d = (1 - way) // 2
        return pltpu.make_async_remote_copy(
            src_ref=steps_ref.at[slot] if s == 0 else place(slot, owner),
            dst_ref=place(slot, owner),
            send_sem=gsend.at[d, slot, s],
            recv_sem=grecv.at[d, slot, s],
            device_id={"space": z + way},
            device_id_type=MESH,
        )

    def sends(s, way):
        if way > 0:
            return (z >= s) & (z < nz - 1)
        return (z + s < nz) & (z > 0)

    def receives(s, way):
        return z - 1 >= s if way > 0 else z + 1 + s < nz

    def arrival(slot, s, way):
        owner = z - way * (s + 1)
        d = (1 - way) // 2
        return pltpu.make_async_remote_copy(
            src_ref=place(slot, owner),
            dst_ref=place(slot, owner),
            send_sem=gsend.at[d, slot, s],
            recv_sem=grecv.at[d, slot, s],
            device_id={"space": z - way},
            device_id_type=MESH,
        )

    def launch(slot, s):
        for way in (1, -1):

            @pl.when(sends(s, way))
            def _():
                hop(slot, s, way).start()

    order = list(range(cap - 1, -1, -1))
    launch(order[0], 0)
    for i, slot in enumerate(order):
        if i + 1 < cap:
            launch(order[i + 1], 0)
        place(slot, z)[...] = steps_ref[slot]
        for s in range(nz - 1):
            for way in (1, -1):

                @pl.when(receives(s, way))
                def _():
                    arrival(slot, s, way).wait_recv()

                if s + 1 < nz - 1:

                    @pl.when(sends(s + 1, way))
                    def _():
                        hop(slot, s + 1, way).start()

    @pl.when(t == nt - 1)
    def _():
        carry[...] = anchor_ref[...]

    def pass_on(k, device):
        columns = pl.ds(pl.multiple_of(k * chunk, chunk), chunk)
        return pltpu.make_async_remote_copy(
            src_ref=out_ref.at[0, :, columns],
            dst_ref=carry.at[:, columns],
            send_sem=csend.at[k],
            recv_sem=crecv.at[k],
            device_id={"tm": device},
            device_id_type=MESH,
        )

    length = len_ref[0]

    def one_chunk(k, _):
        columns = pl.ds(pl.multiple_of(k * chunk, chunk), chunk)

        @pl.when(t < nt - 1)
        def _():
            pass_on(k, t + 1).wait_recv()

        for slot in order:
            before = carry.at[:, columns] if slot == cap - 1 else out_ref.at[slot + 1, :, columns]
            operand = before[...]
            for r in range(0, nodes, tile):
                value = jnp.dot(
                    full[slot, r : r + tile, :], operand, preferred_element_type=jnp.float32
                )
                kept = before[r : r + tile, :].astype(jnp.float32)
                value = jnp.where(slot < length, value, kept)
                out_ref[slot, r : r + tile, columns] = value.astype(out_ref.dtype)

        @pl.when(t > 0)
        def _():
            pass_on(k, t - 1).start()

        return 0

    lax.fori_loop(0, width // chunk, one_chunk, 0)

    for slot in order:
        for s in range(nz - 1):
            for way in (1, -1):

                @pl.when(sends(s, way))
                def _():
                    hop(slot, s, way).wait_send()

    @pl.when(t > 0)
    def _():
        for k in range(width // chunk):
            pass_on(k, t - 1).wait_send()


def shards(nt, nz, steps, lengths, anchor):
    cap, rows, nodes = steps.shape
    width = anchor.shape[1]
    chunks = width // min(CHUNK, width)
    vmem = pl.BlockSpec(memory_space=pltpu.VMEM)
    panels = pl.pallas_call(
        functools.partial(kernel, nt, nz),
        out_shape=jax.ShapeDtypeStruct((cap, nodes, width), jnp.bfloat16),
        in_specs=[pl.BlockSpec(memory_space=pltpu.SMEM), vmem, vmem],
        out_specs=vmem,
        scratch_shapes=[
            pltpu.VMEM((cap, nodes, nodes), jnp.bfloat16),
            pltpu.VMEM((nodes, width), jnp.bfloat16),
            pltpu.SemaphoreType.DMA((2, cap, nz - 1)),
            pltpu.SemaphoreType.DMA((2, cap, nz - 1)),
            pltpu.SemaphoreType.DMA((chunks,)),
            pltpu.SemaphoreType.DMA((chunks,)),
        ],
        compiler_params=pltpu.CompilerParams(collective_id=0, has_side_effects=True),
    )(lengths, steps, anchor)
    used = jnp.arange(cap) < lengths[0]
    return jnp.where(used[:, None, None], panels.astype(jnp.float32), 0.0)


def solution(mesh):
    return jax.shard_map(
        functools.partial(shards, mesh.shape["tm"], mesh.shape["space"]),
        mesh=mesh,
        in_specs=(P("tm", "space", None), P("tm"), P(None, "space")),
        out_specs=P("tm", None, "space"),
        check_vma=False,
    )
```

```python
import functools

import jax
import jax.numpy as jnp
from jax import lax
from jax.experimental import pallas as pl
from jax.experimental.pallas import tpu as pltpu
from jax.sharding import PartitionSpec as P

MESH = pl.DeviceIdType.MESH
CHUNK = 128
TILE = 256


def kernel(
    nt, nz, len_ref, steps_ref, anchor_ref, out_ref, full, carry, scout_out, scout_in,
    gsend, grecv, csend, crecv, ssend, srecv, asend
):
    t, z = lax.axis_index("tm"), lax.axis_index("space")
    cap, rows, nodes = steps_ref.shape
    width = anchor_ref.shape[1]
    chunk = min(CHUNK, width)
    tile = min(TILE, nodes)

    barrier = pltpu.get_barrier_semaphore()
    for axis, at, size in (("tm", t, nt), ("space", z, nz)):
        for step in (1, size - 1):
            pl.semaphore_signal(
                barrier,
                inc=1,
                device_id={axis: lax.rem(at + step, size)},
                device_id_type=MESH,
            )
    half = nt // 2
    at_end = (z == 0) | (z == nz - 1)
    scouts = (z == 1) | (z == nz - 2)
    end = jnp.where(z <= 1, 0, nz - 1)
    scout = jnp.where(z <= 1, 1, nz - 2)
    gives, takes = scouts & (t == half), at_end & (t == half - 1)

    @pl.when(gives)
    def _():
        pl.semaphore_signal(
            barrier,
            inc=1,
            device_id={"tm": half - 1, "space": end},
            device_id_type=MESH,
        )

    @pl.when(takes)
    def _():
        pl.semaphore_signal(
            barrier,
            inc=1,
            device_id={"tm": half, "space": scout},
            device_id_type=MESH,
        )

    pl.semaphore_wait(barrier, 4 + jnp.where(gives | takes, 1, 0))

    def stripe(k):
        return pl.ds(pl.multiple_of(k * chunk, chunk), chunk)

    def lend(k, device):
        return pltpu.make_async_remote_copy(
            src_ref=anchor_ref.at[:, stripe(k)],
            dst_ref=scout_in.at[:, stripe(k)],
            send_sem=asend.at[k],
            recv_sem=srecv.at[k],
            device_id={"space": device},
            device_id_type=MESH,
        )

    lends = at_end & (t == nt - 1)
    chunks = width // chunk

    @pl.when(lends)
    def _():
        for k in range(chunks):
            lend(k, scout).start()

    def place(slot, owner):
        return full.at[slot, pl.ds(pl.multiple_of(owner * rows, rows), rows)]

    def hop(slot, s, way):
        owner = z - way * s
        d = (1 - way) // 2
        return pltpu.make_async_remote_copy(
            src_ref=steps_ref.at[slot] if s == 0 else place(slot, owner),
            dst_ref=place(slot, owner),
            send_sem=gsend.at[d, slot, s],
            recv_sem=grecv.at[d, slot, s],
            device_id={"space": z + way},
            device_id_type=MESH,
        )

    def sends(s, way):
        if way > 0:
            return (z >= s) & (z < nz - 1)
        return (z + s < nz) & (z > 0)

    def receives(s, way):
        return z - 1 >= s if way > 0 else z + 1 + s < nz

    def arrival(slot, s, way):
        owner = z - way * (s + 1)
        d = (1 - way) // 2
        return pltpu.make_async_remote_copy(
            src_ref=place(slot, owner),
            dst_ref=place(slot, owner),
            send_sem=gsend.at[d, slot, s],
            recv_sem=grecv.at[d, slot, s],
            device_id={"space": z - way},
            device_id_type=MESH,
        )

    def launch(slot, s):
        for way in (1, -1):

            @pl.when(sends(s, way))
            def _():
                hop(slot, s, way).start()

    order = list(range(cap - 1, -1, -1))
    launch(order[0], 0)
    for i, slot in enumerate(order):
        if i + 1 < cap:
            launch(order[i + 1], 0)
        place(slot, z)[...] = steps_ref[slot]
        for s in range(nz - 1):
            for way in (1, -1):

                @pl.when(receives(s, way))
                def _():
                    arrival(slot, s, way).wait_recv()

                if s + 1 < nz - 1:

                    @pl.when(sends(s + 1, way))
                    def _():
                        hop(slot, s + 1, way).start()

    @pl.when(t == nt - 1)
    def _():
        carry[...] = anchor_ref[...]

    def pass_on(k, device):
        return pltpu.make_async_remote_copy(
            src_ref=out_ref.at[0, :, stripe(k)],
            dst_ref=carry.at[:, stripe(k)],
            send_sem=csend.at[k],
            recv_sem=crecv.at[k],
            device_id={"tm": device},
            device_id_type=MESH,
        )

    def scout_on(k, device):
        return pltpu.make_async_remote_copy(
            src_ref=scout_out.at[0, :, stripe(k)],
            dst_ref=scout_in.at[:, stripe(k)],
            send_sem=ssend.at[k],
            recv_sem=srecv.at[k],
            device_id={"tm": device},
            device_id_type=MESH,
        )

    def hand_over(k):
        return pltpu.make_async_remote_copy(
            src_ref=scout_out.at[0, :, stripe(k)],
            dst_ref=carry.at[:, stripe(k)],
            send_sem=ssend.at[k],
            recv_sem=crecv.at[k],
            device_id={"tm": half - 1, "space": end},
            device_id_type=MESH,
        )

    length = len_ref[0]

    def days(k, source, result):
        columns = stripe(k)
        for slot in order:
            before = source.at[:, columns] if slot == cap - 1 else result.at[slot + 1, :, columns]
            operand = before[...]
            for r in range(0, nodes, tile):
                value = jnp.dot(
                    full[slot, r : r + tile, :], operand, preferred_element_type=jnp.float32
                )
                kept = before[r : r + tile, :].astype(jnp.float32)
                value = jnp.where(slot < length, value, kept)
                result[slot, r : r + tile, columns] = value.astype(result.dtype)

    @pl.when(scouts & (t >= half))
    def _():
        def scout_chunk(k, _):
            scout_on(k, t - 1).wait_recv()
            days(k, scout_in, scout_out)

            @pl.when(t > half)
            def _():
                scout_on(k, t - 1).start()

            @pl.when(t == half)
            def _():
                hand_over(k).start()

            return 0

        lax.fori_loop(0, chunks, scout_chunk, 0)

    passes = (t > 0) & jnp.logical_not(at_end & (t == half))

    def one_chunk(k, _):
        @pl.when(t < nt - 1)
        def _():
            pass_on(k, t + 1).wait_recv()

        days(k, carry, out_ref)

        @pl.when(passes)
        def _():
            pass_on(k, t - 1).start()

        return 0

    lax.fori_loop(0, chunks, one_chunk, 0)

    @pl.when(lends)
    def _():
        for k in range(chunks):
            lend(k, scout).wait_send()

    @pl.when(scouts & (t > half))
    def _():
        for k in range(chunks):
            scout_on(k, t - 1).wait_send()

    @pl.when(gives)
    def _():
        for k in range(chunks):
            hand_over(k).wait_send()

    for slot in order:
        for s in range(nz - 1):
            for way in (1, -1):

                @pl.when(sends(s, way))
                def _():
                    hop(slot, s, way).wait_send()

    @pl.when(passes)
    def _():
        for k in range(chunks):
            pass_on(k, t - 1).wait_send()


def shards(nt, nz, steps, lengths, anchor):
    cap, rows, nodes = steps.shape
    width = anchor.shape[1]
    chunks = width // min(CHUNK, width)
    vmem = pl.BlockSpec(memory_space=pltpu.VMEM)
    panels = pl.pallas_call(
        functools.partial(kernel, nt, nz),
        out_shape=jax.ShapeDtypeStruct((cap, nodes, width), jnp.bfloat16),
        in_specs=[pl.BlockSpec(memory_space=pltpu.SMEM), vmem, vmem],
        out_specs=vmem,
        scratch_shapes=[
            pltpu.VMEM((cap, nodes, nodes), jnp.bfloat16),
            pltpu.VMEM((nodes, width), jnp.bfloat16),
            pltpu.VMEM((cap, nodes, width), jnp.bfloat16),
            pltpu.VMEM((nodes, width), jnp.bfloat16),
            pltpu.SemaphoreType.DMA((2, cap, nz - 1)),
            pltpu.SemaphoreType.DMA((2, cap, nz - 1)),
            pltpu.SemaphoreType.DMA((chunks,)),
            pltpu.SemaphoreType.DMA((chunks,)),
            pltpu.SemaphoreType.DMA((chunks,)),
            pltpu.SemaphoreType.DMA((chunks,)),
            pltpu.SemaphoreType.DMA((chunks,)),
        ],
        compiler_params=pltpu.CompilerParams(collective_id=0, has_side_effects=True),
    )(lengths, steps, anchor)
    used = jnp.arange(cap) < lengths[0]
    return jnp.where(used[:, None, None], panels.astype(jnp.float32), 0.0)


def solution(mesh):
    return jax.shard_map(
        functools.partial(shards, mesh.shape["tm"], mesh.shape["space"]),
        mesh=mesh,
        in_specs=(P("tm", "space", None), P("tm"), P(None, "space")),
        out_specs=P("tm", None, "space"),
        check_vma=False,
    )
```

```python
import functools

import jax
import jax.numpy as jnp
from jax import lax
from jax.experimental import pallas as pl
from jax.experimental.pallas import tpu as pltpu
from jax.sharding import PartitionSpec as P

MESH = pl.DeviceIdType.MESH
CHUNK = 128
TILE = 256
SPANS = 2


def kernel(
    nt, nz, len_ref, steps_ref, anchor_ref, out_ref, full, carry, scout_out, scout_in,
    gsend, grecv, csend, crecv, ssend, srecv, asend, hsend
):
    t, z = lax.axis_index("tm"), lax.axis_index("space")
    cap, rows, nodes = steps_ref.shape
    width = anchor_ref.shape[1]
    chunk = min(CHUNK, width)
    tile = min(TILE, nodes)

    barrier = pltpu.get_barrier_semaphore()
    for axis, at, size in (("tm", t, nt), ("space", z, nz)):
        for step in (1, size - 1):
            pl.semaphore_signal(
                barrier,
                inc=1,
                device_id={axis: lax.rem(at + step, size)},
                device_id_type=MESH,
            )
    span = nt // SPANS
    at_end = (z == 0) | (z == nz - 1)
    scouts = (z == 1) | (z == nz - 2)
    end = jnp.where(z <= 1, 0, nz - 1)
    scout = jnp.where(z <= 1, 1, nz - 2)
    edge = lax.rem(t, span) == 0
    gives = scouts & edge & (t > 0)
    takes = at_end & (lax.rem(t, span) == span - 1) & (t < nt - 1)

    @pl.when(gives)
    def _():
        pl.semaphore_signal(
            barrier,
            inc=1,
            device_id={"tm": t - 1, "space": end},
            device_id_type=MESH,
        )

    @pl.when(takes)
    def _():
        pl.semaphore_signal(
            barrier,
            inc=1,
            device_id={"tm": t + 1, "space": scout},
            device_id_type=MESH,
        )

    pl.semaphore_wait(barrier, 4 + jnp.where(gives | takes, 1, 0))

    def stripe(k):
        return pl.ds(pl.multiple_of(k * chunk, chunk), chunk)

    def lend(k, device):
        return pltpu.make_async_remote_copy(
            src_ref=anchor_ref.at[:, stripe(k)],
            dst_ref=scout_in.at[:, stripe(k)],
            send_sem=asend.at[k],
            recv_sem=srecv.at[k],
            device_id={"space": device},
            device_id_type=MESH,
        )

    lends = at_end & (t == nt - 1)
    chunks = width // chunk

    @pl.when(lends)
    def _():
        for k in range(chunks):
            lend(k, scout).start()

    order = list(range(cap - 1, -1, -1))
    length = len_ref[0]
    pair = 2 if chunks % 2 == 0 else 1

    def days(k, count, source, result, slots):
        columns = pl.ds(pl.multiple_of(k * chunk, chunk), count * chunk)
        for slot in slots:
            before = source.at[:, columns] if slot == cap - 1 else result.at[slot + 1, :, columns]
            operand = before[...]
            for r in range(0, nodes, tile):
                value = jnp.dot(
                    full[slot, r : r + tile, :], operand, preferred_element_type=jnp.float32
                )
                kept = before[r : r + tile, :].astype(jnp.float32)
                value = jnp.where(slot < length, value, kept)
                result[slot, r : r + tile, columns] = value.astype(result.dtype)

    @pl.when(t == nt - 1)
    def _():
        carry[...] = anchor_ref[...]

    def place(slot, owner):
        return full.at[slot, pl.ds(pl.multiple_of(owner * rows, rows), rows)]

    def hop(slot, s, way):
        owner = z - way * s
        d = (1 - way) // 2
        return pltpu.make_async_remote_copy(
            src_ref=steps_ref.at[slot] if s == 0 else place(slot, owner),
            dst_ref=place(slot, owner),
            send_sem=gsend.at[d, slot, s],
            recv_sem=grecv.at[d, slot, s],
            device_id={"space": z + way},
            device_id_type=MESH,
        )

    def sends(s, way):
        if way > 0:
            return (z >= s) & (z < nz - 1)
        return (z + s < nz) & (z > 0)

    def receives(s, way):
        return z - 1 >= s if way > 0 else z + 1 + s < nz

    def arrival(slot, s, way):
        owner = z - way * (s + 1)
        d = (1 - way) // 2
        return pltpu.make_async_remote_copy(
            src_ref=place(slot, owner),
            dst_ref=place(slot, owner),
            send_sem=gsend.at[d, slot, s],
            recv_sem=grecv.at[d, slot, s],
            device_id={"space": z - way},
            device_id_type=MESH,
        )

    def launch(slot, s):
        for way in (1, -1):

            @pl.when(sends(s, way))
            def _():
                hop(slot, s, way).start()

    launch(order[0], 0)
    for i, slot in enumerate(order):
        if i + 1 < cap:
            launch(order[i + 1], 0)
        place(slot, z)[...] = steps_ref[slot]
        for s in range(nz - 1):
            for way in (1, -1):

                @pl.when(receives(s, way))
                def _():
                    arrival(slot, s, way).wait_recv()

                if s + 1 < nz - 1:

                    @pl.when(sends(s + 1, way))
                    def _():
                        hop(slot, s + 1, way).start()

        if slot > 0:
            @pl.when(t == nt - 1)
            def _():
                def early(k, _):
                    days(k * pair, pair, carry, out_ref, [slot])
                    return 0

                lax.fori_loop(0, chunks // pair, early, 0)

    def pass_on(k, device):
        return pltpu.make_async_remote_copy(
            src_ref=out_ref.at[0, :, stripe(k)],
            dst_ref=carry.at[:, stripe(k)],
            send_sem=csend.at[k],
            recv_sem=crecv.at[k],
            device_id={"tm": device},
            device_id_type=MESH,
        )

    def scout_on(k, device):
        return pltpu.make_async_remote_copy(
            src_ref=scout_out.at[0, :, stripe(k)],
            dst_ref=scout_in.at[:, stripe(k)],
            send_sem=ssend.at[k],
            recv_sem=srecv.at[k],
            device_id={"tm": device},
            device_id_type=MESH,
        )

    def hand_over(k):
        return pltpu.make_async_remote_copy(
            src_ref=scout_out.at[0, :, stripe(k)],
            dst_ref=carry.at[:, stripe(k)],
            send_sem=hsend.at[k],
            recv_sem=crecv.at[k],
            device_id={"tm": t - 1, "space": end},
            device_id_type=MESH,
        )

    @pl.when(scouts & (t >= span))
    def _():
        def scout_chunk(j, _):
            for k in range(pair):
                scout_on(j * pair + k, t - 1).wait_recv()
            days(j * pair, pair, scout_in, scout_out, order)
            for k in range(pair):

                @pl.when(edge)
                def _():
                    hand_over(j * pair + k).start()

                @pl.when(t > span)
                def _():
                    scout_on(j * pair + k, t - 1).start()

            return 0

        lax.fori_loop(0, chunks // pair, scout_chunk, 0)

    passes = (t > 0) & jnp.logical_not(at_end & edge)

    def chain(count):
        def one_chunk(j, _):
            @pl.when(t < nt - 1)
            def _():
                for k in range(count):
                    pass_on(j * count + k, t + 1).wait_recv()
                days(j * count, count, carry, out_ref, order)

            @pl.when(t == nt - 1)
            def _():
                days(j * count, count, carry, out_ref, order[-1:])

            @pl.when(passes)
            def _():
                for k in range(count):
                    pass_on(j * count + k, t - 1).start()

            return 0

        lax.fori_loop(0, chunks // count, one_chunk, 0)

    @pl.when(at_end)
    def _():
        chain(1)

    @pl.when(jnp.logical_not(at_end))
    def _():
        chain(pair)

    @pl.when(lends)
    def _():
        for k in range(chunks):
            lend(k, scout).wait_send()

    @pl.when(scouts & (t > span))
    def _():
        for k in range(chunks):
            scout_on(k, t - 1).wait_send()

    @pl.when(gives)
    def _():
        for k in range(chunks):
            hand_over(k).wait_send()

    for slot in order:
        for s in range(nz - 1):
            for way in (1, -1):

                @pl.when(sends(s, way))
                def _():
                    hop(slot, s, way).wait_send()

    @pl.when(passes)
    def _():
        for k in range(chunks):
            pass_on(k, t - 1).wait_send()


def shards(nt, nz, steps, lengths, anchor):
    cap, rows, nodes = steps.shape
    width = anchor.shape[1]
    chunks = width // min(CHUNK, width)
    vmem = pl.BlockSpec(memory_space=pltpu.VMEM)
    panels = pl.pallas_call(
        functools.partial(kernel, nt, nz),
        out_shape=jax.ShapeDtypeStruct((cap, nodes, width), jnp.bfloat16),
        in_specs=[pl.BlockSpec(memory_space=pltpu.SMEM), vmem, vmem],
        out_specs=vmem,
        scratch_shapes=[
            pltpu.VMEM((cap, nodes, nodes), jnp.bfloat16),
            pltpu.VMEM((nodes, width), jnp.bfloat16),
            pltpu.VMEM((cap, nodes, width), jnp.bfloat16),
            pltpu.VMEM((nodes, width), jnp.bfloat16),
            pltpu.SemaphoreType.DMA((2, cap, nz - 1)),
            pltpu.SemaphoreType.DMA((2, cap, nz - 1)),
            pltpu.SemaphoreType.DMA((chunks,)),
            pltpu.SemaphoreType.DMA((chunks,)),
            pltpu.SemaphoreType.DMA((chunks,)),
            pltpu.SemaphoreType.DMA((chunks,)),
            pltpu.SemaphoreType.DMA((chunks,)),
            pltpu.SemaphoreType.DMA((chunks,)),
        ],
        compiler_params=pltpu.CompilerParams(collective_id=0, has_side_effects=True),
    )(lengths, steps, anchor)
    used = jnp.arange(cap) < lengths[0]
    return jnp.where(used[:, None, None], panels.astype(jnp.float32), 0.0)


def solution(mesh):
    return jax.shard_map(
        functools.partial(shards, mesh.shape["tm"], mesh.shape["space"]),
        mesh=mesh,
        in_specs=(P("tm", "space", None), P("tm"), P(None, "space")),
        out_specs=P("tm", None, "space"),
        check_vma=False,
    )
```

```python
import functools

import jax
import jax.numpy as jnp
from jax import lax
from jax.experimental import pallas as pl
from jax.experimental.pallas import tpu as pltpu
from jax.sharding import PartitionSpec as P

MESH = pl.DeviceIdType.MESH
CHUNK = 128
TILE = 256
SPANS = 4


def kernel(
    nt, nz, len_ref, steps_ref, anchor_ref, out_ref, full, carry, scout_out, scout_in,
    gsend, grecv, csend, crecv, ssend, srecv, asend, hsend
):
    t, z = lax.axis_index("tm"), lax.axis_index("space")
    cap, rows, nodes = steps_ref.shape
    width = anchor_ref.shape[1]
    chunk = min(CHUNK, width)
    tile = min(TILE, nodes)

    barrier = pltpu.get_barrier_semaphore()
    for axis, at, size in (("tm", t, nt), ("space", z, nz)):
        for step in (1, size - 1):
            pl.semaphore_signal(
                barrier,
                inc=1,
                device_id={axis: lax.rem(at + step, size)},
                device_id_type=MESH,
            )
    span = max(1, nt // SPANS)
    at_end = (z == 0) | (z == nz - 1)
    scouts = (z == 1) | (z == nz - 2)
    end = jnp.where(z <= 1, 0, nz - 1)
    scout = jnp.where(z <= 1, 1, nz - 2)
    edge = lax.rem(t, span) == 0
    gives = scouts & edge & (t > 0)
    takes = at_end & (lax.rem(t, span) == span - 1) & (t < nt - 1)

    @pl.when(gives)
    def _():
        pl.semaphore_signal(
            barrier,
            inc=1,
            device_id={"tm": t - 1, "space": end},
            device_id_type=MESH,
        )

    @pl.when(takes)
    def _():
        pl.semaphore_signal(
            barrier,
            inc=1,
            device_id={"tm": t + 1, "space": scout},
            device_id_type=MESH,
        )

    pl.semaphore_wait(barrier, 4 + jnp.where(gives | takes, 1, 0))

    def stripe(k):
        return pl.ds(pl.multiple_of(k * chunk, chunk), chunk)

    def lend(k, device):
        return pltpu.make_async_remote_copy(
            src_ref=anchor_ref.at[:, stripe(k)],
            dst_ref=scout_in.at[:, stripe(k)],
            send_sem=asend.at[k],
            recv_sem=srecv.at[k],
            device_id={"space": device},
            device_id_type=MESH,
        )

    lends = at_end & (t == nt - 1)
    chunks = width // chunk

    @pl.when(lends)
    def _():
        for k in range(chunks):
            lend(k, scout).start()

    order = list(range(cap - 1, -1, -1))
    length = len_ref[0]
    pair = 2 if chunks % 2 == 0 else 1

    def days(k, count, source, result, slots):
        columns = pl.ds(pl.multiple_of(k * chunk, chunk), count * chunk)
        for slot in slots:
            before = source.at[:, columns] if slot == cap - 1 else result.at[slot + 1, :, columns]
            operand = before[...]
            for r in range(0, nodes, tile):
                value = jnp.dot(
                    full[slot, r : r + tile, :], operand, preferred_element_type=jnp.float32
                )
                kept = before[r : r + tile, :].astype(jnp.float32)
                value = jnp.where(slot < length, value, kept)
                result[slot, r : r + tile, columns] = value.astype(result.dtype)

    @pl.when(t == nt - 1)
    def _():
        carry[...] = anchor_ref[...]

    def place(slot, owner):
        return full.at[slot, pl.ds(pl.multiple_of(owner * rows, rows), rows)]

    def hop(slot, s, way):
        owner = z - way * s
        d = (1 - way) // 2
        return pltpu.make_async_remote_copy(
            src_ref=steps_ref.at[slot] if s == 0 else place(slot, owner),
            dst_ref=place(slot, owner),
            send_sem=gsend.at[d, slot, s],
            recv_sem=grecv.at[d, slot, s],
            device_id={"space": z + way},
            device_id_type=MESH,
        )

    def sends(s, way):
        if way > 0:
            return (z >= s) & (z < nz - 1)
        return (z + s < nz) & (z > 0)

    def receives(s, way):
        return z - 1 >= s if way > 0 else z + 1 + s < nz

    def arrival(slot, s, way):
        owner = z - way * (s + 1)
        d = (1 - way) // 2
        return pltpu.make_async_remote_copy(
            src_ref=place(slot, owner),
            dst_ref=place(slot, owner),
            send_sem=gsend.at[d, slot, s],
            recv_sem=grecv.at[d, slot, s],
            device_id={"space": z - way},
            device_id_type=MESH,
        )

    def launch(slot, s):
        for way in (1, -1):

            @pl.when(sends(s, way))
            def _():
                hop(slot, s, way).start()

    launch(order[0], 0)
    for i, slot in enumerate(order):
        if i + 1 < cap:
            launch(order[i + 1], 0)
        place(slot, z)[...] = steps_ref[slot]
        for s in range(nz - 1):
            for way in (1, -1):

                @pl.when(receives(s, way))
                def _():
                    arrival(slot, s, way).wait_recv()

                if s + 1 < nz - 1:

                    @pl.when(sends(s + 1, way))
                    def _():
                        hop(slot, s + 1, way).start()

        if slot > 0:
            @pl.when(t == nt - 1)
            def _():
                def early(k, _):
                    days(k * pair, pair, carry, out_ref, [slot])
                    return 0

                lax.fori_loop(0, chunks // pair, early, 0)

    def pass_on(k, device):
        return pltpu.make_async_remote_copy(
            src_ref=out_ref.at[0, :, stripe(k)],
            dst_ref=carry.at[:, stripe(k)],
            send_sem=csend.at[k],
            recv_sem=crecv.at[k],
            device_id={"tm": device},
            device_id_type=MESH,
        )

    def scout_on(k, device):
        return pltpu.make_async_remote_copy(
            src_ref=scout_out.at[0, :, stripe(k)],
            dst_ref=scout_in.at[:, stripe(k)],
            send_sem=ssend.at[k],
            recv_sem=srecv.at[k],
            device_id={"tm": device},
            device_id_type=MESH,
        )

    def hand_over(k):
        return pltpu.make_async_remote_copy(
            src_ref=scout_out.at[0, :, stripe(k)],
            dst_ref=carry.at[:, stripe(k)],
            send_sem=hsend.at[k],
            recv_sem=crecv.at[k],
            device_id={"tm": t - 1, "space": end},
            device_id_type=MESH,
        )

    @pl.when(scouts & (t >= span))
    def _():
        def scout_chunk(k, _):
            scout_on(k, t - 1).wait_recv()
            days(k, 1, scout_in, scout_out, order)

            @pl.when(edge)
            def _():
                hand_over(k).start()

            @pl.when(t > span)
            def _():
                scout_on(k, t - 1).start()

            return 0

        lax.fori_loop(0, chunks, scout_chunk, 0)

    passes = (t > 0) & jnp.logical_not(at_end & edge)

    def chain(count):
        def one_chunk(j, _):
            @pl.when(t < nt - 1)
            def _():
                for k in range(count):
                    pass_on(j * count + k, t + 1).wait_recv()
                days(j * count, count, carry, out_ref, order)

            @pl.when(t == nt - 1)
            def _():
                days(j * count, count, carry, out_ref, order[-1:])

            @pl.when(passes)
            def _():
                for k in range(count):
                    pass_on(j * count + k, t - 1).start()

            return 0

        lax.fori_loop(0, chunks // count, one_chunk, 0)

    @pl.when(at_end)
    def _():
        chain(pair)

    @pl.when(jnp.logical_not(at_end))
    def _():
        chain(1)

    @pl.when(lends)
    def _():
        for k in range(chunks):
            lend(k, scout).wait_send()

    @pl.when(scouts & (t > span))
    def _():
        for k in range(chunks):
            scout_on(k, t - 1).wait_send()

    @pl.when(gives)
    def _():
        for k in range(chunks):
            hand_over(k).wait_send()

    for slot in order:
        for s in range(nz - 1):
            for way in (1, -1):

                @pl.when(sends(s, way))
                def _():
                    hop(slot, s, way).wait_send()

    @pl.when(passes)
    def _():
        for k in range(chunks):
            pass_on(k, t - 1).wait_send()


def shards(nt, nz, steps, lengths, anchor):
    cap, rows, nodes = steps.shape
    width = anchor.shape[1]
    chunks = width // min(CHUNK, width)
    vmem = pl.BlockSpec(memory_space=pltpu.VMEM)
    panels = pl.pallas_call(
        functools.partial(kernel, nt, nz),
        out_shape=jax.ShapeDtypeStruct((cap, nodes, width), jnp.bfloat16),
        in_specs=[pl.BlockSpec(memory_space=pltpu.SMEM), vmem, vmem],
        out_specs=vmem,
        scratch_shapes=[
            pltpu.VMEM((cap, nodes, nodes), jnp.bfloat16),
            pltpu.VMEM((nodes, width), jnp.bfloat16),
            pltpu.VMEM((cap, nodes, width), jnp.bfloat16),
            pltpu.VMEM((nodes, width), jnp.bfloat16),
            pltpu.SemaphoreType.DMA((2, cap, nz - 1)),
            pltpu.SemaphoreType.DMA((2, cap, nz - 1)),
            pltpu.SemaphoreType.DMA((chunks,)),
            pltpu.SemaphoreType.DMA((chunks,)),
            pltpu.SemaphoreType.DMA((chunks,)),
            pltpu.SemaphoreType.DMA((chunks,)),
            pltpu.SemaphoreType.DMA((chunks,)),
            pltpu.SemaphoreType.DMA((chunks,)),
        ],
        compiler_params=pltpu.CompilerParams(collective_id=0, has_side_effects=True),
    )(lengths, steps, anchor)
    used = jnp.arange(cap) < lengths[0]
    return jnp.where(used[:, None, None], panels.astype(jnp.float32), 0.0)


def solution(mesh):
    return jax.shard_map(
        functools.partial(shards, mesh.shape["tm"], mesh.shape["space"]),
        mesh=mesh,
        in_specs=(P("tm", "space", None), P("tm"), P(None, "space")),
        out_specs=P("tm", None, "space"),
        check_vma=False,
    )
```

```python
import functools

import jax
import jax.numpy as jnp
from jax import lax
from jax.experimental import pallas as pl
from jax.experimental.pallas import tpu as pltpu
from jax.sharding import PartitionSpec as P

MESH = pl.DeviceIdType.MESH
CHUNK = 128
TILE = 256
SPANS = 4


def kernel(
    nt, nz, len_ref, steps_ref, anchor_ref, out_ref, full, carry, scout_out, scout_in,
    gsend, grecv, csend, crecv, ssend, srecv, asend, hsend
):
    t, z = lax.axis_index("tm"), lax.axis_index("space")
    cap, rows, nodes = steps_ref.shape
    width = anchor_ref.shape[1]
    chunk = min(CHUNK, width)
    tile = min(TILE, nodes)

    barrier = pltpu.get_barrier_semaphore()
    for axis, at, size in (("tm", t, nt), ("space", z, nz)):
        for step in (1, size - 1):
            pl.semaphore_signal(
                barrier,
                inc=1,
                device_id={axis: lax.rem(at + step, size)},
                device_id_type=MESH,
            )
    span = max(1, nt // SPANS)
    at_end = (z == 0) | (z == nz - 1)
    scouts = (z == 1) | (z == nz - 2)
    end = jnp.where(z <= 1, 0, nz - 1)
    scout = jnp.where(z <= 1, 1, nz - 2)
    edge = lax.rem(t, span) == 0
    gives = scouts & edge & (t > 0)
    takes = at_end & (lax.rem(t, span) == span - 1) & (t < nt - 1)

    @pl.when(gives)
    def _():
        pl.semaphore_signal(
            barrier,
            inc=1,
            device_id={"tm": t - 1, "space": end},
            device_id_type=MESH,
        )

    @pl.when(takes)
    def _():
        pl.semaphore_signal(
            barrier,
            inc=1,
            device_id={"tm": t + 1, "space": scout},
            device_id_type=MESH,
        )

    pl.semaphore_wait(barrier, 4 + jnp.where(gives | takes, 1, 0))

    def stripe(k):
        return pl.ds(pl.multiple_of(k * chunk, chunk), chunk)

    def lend(k, device):
        return pltpu.make_async_remote_copy(
            src_ref=anchor_ref.at[:, stripe(k)],
            dst_ref=scout_in.at[:, stripe(k)],
            send_sem=asend.at[k],
            recv_sem=srecv.at[k],
            device_id={"space": device},
            device_id_type=MESH,
        )

    lends = at_end & (t == nt - 1)
    chunks = width // chunk

    @pl.when(lends)
    def _():
        for k in range(chunks):
            lend(k, scout).start()

    order = list(range(cap - 1, -1, -1))
    length = len_ref[0]
    pair = 2 if chunks % 2 == 0 else 1

    def days(k, count, source, result, slots):
        columns = pl.ds(pl.multiple_of(k * chunk, chunk), count * chunk)
        for slot in slots:
            before = source.at[:, columns] if slot == cap - 1 else result.at[slot + 1, :, columns]
            operand = before[...]
            for r in range(0, nodes, tile):
                value = jnp.dot(
                    full[slot, r : r + tile, :], operand, preferred_element_type=jnp.float32
                )
                kept = before[r : r + tile, :].astype(jnp.float32)
                value = jnp.where(slot < length, value, kept)
                result[slot, r : r + tile, columns] = value.astype(result.dtype)

    @pl.when(t == nt - 1)
    def _():
        carry[...] = anchor_ref[...]

    def place(slot, owner):
        return full.at[slot, pl.ds(pl.multiple_of(owner * rows, rows), rows)]

    def hop(slot, s, way):
        owner = z - way * s
        d = (1 - way) // 2
        return pltpu.make_async_remote_copy(
            src_ref=steps_ref.at[slot] if s == 0 else place(slot, owner),
            dst_ref=place(slot, owner),
            send_sem=gsend.at[d, slot, s],
            recv_sem=grecv.at[d, slot, s],
            device_id={"space": z + way},
            device_id_type=MESH,
        )

    def sends(s, way):
        if way > 0:
            return (z >= s) & (z < nz - 1)
        return (z + s < nz) & (z > 0)

    def receives(s, way):
        return z - 1 >= s if way > 0 else z + 1 + s < nz

    def arrival(slot, s, way):
        owner = z - way * (s + 1)
        d = (1 - way) // 2
        return pltpu.make_async_remote_copy(
            src_ref=place(slot, owner),
            dst_ref=place(slot, owner),
            send_sem=gsend.at[d, slot, s],
            recv_sem=grecv.at[d, slot, s],
            device_id={"space": z - way},
            device_id_type=MESH,
        )

    def launch(slot, s):
        for way in (1, -1):

            @pl.when(sends(s, way))
            def _():
                hop(slot, s, way).start()

    launch(order[0], 0)
    for i, slot in enumerate(order):
        if i + 1 < cap:
            launch(order[i + 1], 0)
        place(slot, z)[...] = steps_ref[slot]
        for s in range(nz - 1):
            for way in (1, -1):

                @pl.when(receives(s, way))
                def _():
                    arrival(slot, s, way).wait_recv()

                if s + 1 < nz - 1:

                    @pl.when(sends(s + 1, way))
                    def _():
                        hop(slot, s + 1, way).start()

        if slot > 0:
            @pl.when(at_end & (t == nt - 1))
            def _():
                def early(k, _):
                    days(k * pair, pair, carry, out_ref, [slot])
                    return 0

                lax.fori_loop(0, chunks // pair, early, 0)

    def pass_on(k, device):
        return pltpu.make_async_remote_copy(
            src_ref=out_ref.at[0, :, stripe(k)],
            dst_ref=carry.at[:, stripe(k)],
            send_sem=csend.at[k],
            recv_sem=crecv.at[k],
            device_id={"tm": device},
            device_id_type=MESH,
        )

    def scout_on(k, device):
        return pltpu.make_async_remote_copy(
            src_ref=scout_out.at[0, :, stripe(k)],
            dst_ref=scout_in.at[:, stripe(k)],
            send_sem=ssend.at[k],
            recv_sem=srecv.at[k],
            device_id={"tm": device},
            device_id_type=MESH,
        )

    def hand_over(k):
        return pltpu.make_async_remote_copy(
            src_ref=scout_out.at[0, :, stripe(k)],
            dst_ref=carry.at[:, stripe(k)],
            send_sem=hsend.at[k],
            recv_sem=crecv.at[k],
            device_id={"tm": t - 1, "space": end},
            device_id_type=MESH,
        )

    def both_days(k):
        columns = stripe(k)
        for slot in order:
            if slot == cap - 1:
                mine, other = carry.at[:, columns], scout_in.at[:, columns]
            else:
                mine = out_ref.at[slot + 1, :, columns]
                other = scout_out.at[slot + 1, :, columns]
            operand = jnp.concatenate([mine[...], other[...]], axis=1)
            for r in range(0, nodes, tile):
                values = jnp.dot(
                    full[slot, r : r + tile, :], operand, preferred_element_type=jnp.float32
                )
                for i, (before, result) in enumerate(((mine, out_ref), (other, scout_out))):
                    value = values[:, i * chunk : (i + 1) * chunk]
                    kept = before[r : r + tile, :].astype(jnp.float32)
                    value = jnp.where(slot < length, value, kept)
                    result[slot, r : r + tile, columns] = value.astype(result.dtype)

    leads = scouts & (t >= span)

    @pl.when(leads)
    def _():
        def scout_chunk(k, _):
            @pl.when(t < nt - 1)
            def _():
                pass_on(k, t + 1).wait_recv()

            scout_on(k, t - 1).wait_recv()
            both_days(k)
            pass_on(k, t - 1).start()

            @pl.when(edge)
            def _():
                hand_over(k).start()

            @pl.when(t > span)
            def _():
                scout_on(k, t - 1).start()

            return 0

        lax.fori_loop(0, chunks, scout_chunk, 0)

    passes = (t > 0) & jnp.logical_not(at_end & edge)

    def chain(count):
        def one_chunk(j, _):
            @pl.when(t < nt - 1)
            def _():
                for k in range(count):
                    pass_on(j * count + k, t + 1).wait_recv()

            @pl.when(jnp.logical_not(at_end & (t == nt - 1)))
            def _():
                days(j * count, count, carry, out_ref, order)

            @pl.when(at_end & (t == nt - 1))
            def _():
                days(j * count, count, carry, out_ref, order[-1:])

            @pl.when(passes)
            def _():
                for k in range(count):
                    pass_on(j * count + k, t - 1).start()

            return 0

        lax.fori_loop(0, chunks // count, one_chunk, 0)

    @pl.when(at_end)
    def _():
        chain(pair)

    @pl.when(jnp.logical_not(at_end | leads))
    def _():
        chain(1)

    @pl.when(lends)
    def _():
        for k in range(chunks):
            lend(k, scout).wait_send()

    @pl.when(scouts & (t > span))
    def _():
        for k in range(chunks):
            scout_on(k, t - 1).wait_send()

    @pl.when(gives)
    def _():
        for k in range(chunks):
            hand_over(k).wait_send()

    for slot in order:
        for s in range(nz - 1):
            for way in (1, -1):

                @pl.when(sends(s, way))
                def _():
                    hop(slot, s, way).wait_send()

    @pl.when(passes)
    def _():
        for k in range(chunks):
            pass_on(k, t - 1).wait_send()


def shards(nt, nz, steps, lengths, anchor):
    cap, rows, nodes = steps.shape
    width = anchor.shape[1]
    chunks = width // min(CHUNK, width)
    vmem = pl.BlockSpec(memory_space=pltpu.VMEM)
    panels = pl.pallas_call(
        functools.partial(kernel, nt, nz),
        out_shape=jax.ShapeDtypeStruct((cap, nodes, width), jnp.bfloat16),
        in_specs=[pl.BlockSpec(memory_space=pltpu.SMEM), vmem, vmem],
        out_specs=vmem,
        scratch_shapes=[
            pltpu.VMEM((cap, nodes, nodes), jnp.bfloat16),
            pltpu.VMEM((nodes, width), jnp.bfloat16),
            pltpu.VMEM((cap, nodes, width), jnp.bfloat16),
            pltpu.VMEM((nodes, width), jnp.bfloat16),
            pltpu.SemaphoreType.DMA((2, cap, nz - 1)),
            pltpu.SemaphoreType.DMA((2, cap, nz - 1)),
            pltpu.SemaphoreType.DMA((chunks,)),
            pltpu.SemaphoreType.DMA((chunks,)),
            pltpu.SemaphoreType.DMA((chunks,)),
            pltpu.SemaphoreType.DMA((chunks,)),
            pltpu.SemaphoreType.DMA((chunks,)),
            pltpu.SemaphoreType.DMA((chunks,)),
        ],
        compiler_params=pltpu.CompilerParams(collective_id=0, has_side_effects=True),
    )(lengths, steps, anchor)
    used = jnp.arange(cap) < lengths[0]
    return jnp.where(used[:, None, None], panels.astype(jnp.float32), 0.0)


def solution(mesh):
    return jax.shard_map(
        functools.partial(shards, mesh.shape["tm"], mesh.shape["space"]),
        mesh=mesh,
        in_specs=(P("tm", "space", None), P("tm"), P(None, "space")),
        out_specs=P("tm", None, "space"),
        check_vma=False,
    )
```

```python
import functools

import jax
import jax.numpy as jnp
from jax import lax
from jax.experimental import pallas as pl
from jax.experimental.pallas import tpu as pltpu
from jax.sharding import PartitionSpec as P

MESH = pl.DeviceIdType.MESH
CHUNK = 128
TILE = 256
SPANS = 4
GRANT = 28 << 20


def kernel(
    nt, nz, len_ref, steps_ref, anchor_ref, out_ref, full, carry, scout_out, scout_in,
    gsend, grecv, csend, crecv, ssend, srecv, asend, hsend
):
    t, z = lax.axis_index("tm"), lax.axis_index("space")
    cap, rows, nodes = steps_ref.shape
    width = anchor_ref.shape[1]
    chunk = min(CHUNK, width)
    tile = min(TILE, nodes)

    barrier = pltpu.get_barrier_semaphore()
    for axis, at, size in (("tm", t, nt), ("space", z, nz)):
        for step in (1, size - 1):
            pl.semaphore_signal(
                barrier,
                inc=1,
                device_id={axis: lax.rem(at + step, size)},
                device_id_type=MESH,
            )
    span = max(1, nt // SPANS)
    at_end = (z == 0) | (z == nz - 1)
    scouts = (z == 1) | (z == nz - 2)
    end = jnp.where(z <= 1, 0, nz - 1)
    scout = jnp.where(z <= 1, 1, nz - 2)
    edge = lax.rem(t, span) == 0
    gives = scouts & edge & (t > 0)
    takes = at_end & (lax.rem(t, span) == span - 1) & (t < nt - 1)

    @pl.when(gives)
    def _():
        pl.semaphore_signal(
            barrier,
            inc=1,
            device_id={"tm": t - 1, "space": end},
            device_id_type=MESH,
        )

    @pl.when(takes)
    def _():
        pl.semaphore_signal(
            barrier,
            inc=1,
            device_id={"tm": t + 1, "space": scout},
            device_id_type=MESH,
        )

    pl.semaphore_wait(barrier, 4 + jnp.where(gives | takes, 1, 0))

    def stripe(k):
        return pl.ds(pl.multiple_of(k * chunk, chunk), chunk)

    def lend(k, device):
        return pltpu.make_async_remote_copy(
            src_ref=anchor_ref.at[:, stripe(k)],
            dst_ref=scout_in.at[:, stripe(k)],
            send_sem=asend.at[k],
            recv_sem=srecv.at[k],
            device_id={"space": device},
            device_id_type=MESH,
        )

    lends = at_end & (t == nt - 1)
    chunks = width // chunk

    @pl.when(lends)
    def _():
        for k in range(chunks):
            lend(k, scout).start()

    order = list(range(cap - 1, -1, -1))
    length = len_ref[0]
    pair = 2 if chunks % 2 == 0 else 1

    def days(k, count, source, result, slots):
        columns = pl.ds(pl.multiple_of(k * chunk, chunk), count * chunk)
        for slot in slots:
            before = source.at[:, columns] if slot == cap - 1 else result.at[slot + 1, :, columns]
            operand = before[...]
            for r in range(0, nodes, tile):
                value = jnp.dot(
                    full[slot, r : r + tile, :], operand, preferred_element_type=jnp.float32
                )
                kept = before[r : r + tile, :].astype(jnp.float32)
                value = jnp.where(slot < length, value, kept)
                result[slot, r : r + tile, columns] = value.astype(result.dtype)

    @pl.when(t == nt - 1)
    def _():
        carry[...] = anchor_ref[...]

    def place(slot, owner):
        return full.at[slot, pl.ds(pl.multiple_of(owner * rows, rows), rows)]

    def hop(slot, s, way):
        owner = z - way * s
        d = (1 - way) // 2
        return pltpu.make_async_remote_copy(
            src_ref=steps_ref.at[slot] if s == 0 else place(slot, owner),
            dst_ref=place(slot, owner),
            send_sem=gsend.at[d, slot, s],
            recv_sem=grecv.at[d, slot, s],
            device_id={"space": z + way},
            device_id_type=MESH,
        )

    def sends(s, way):
        if way > 0:
            return (z >= s) & (z < nz - 1)
        return (z + s < nz) & (z > 0)

    def receives(s, way):
        return z - 1 >= s if way > 0 else z + 1 + s < nz

    def arrival(slot, s, way):
        owner = z - way * (s + 1)
        d = (1 - way) // 2
        return pltpu.make_async_remote_copy(
            src_ref=place(slot, owner),
            dst_ref=place(slot, owner),
            send_sem=gsend.at[d, slot, s],
            recv_sem=grecv.at[d, slot, s],
            device_id={"space": z - way},
            device_id_type=MESH,
        )

    def launch(slot, s):
        for way in (1, -1):

            @pl.when(sends(s, way))
            def _():
                hop(slot, s, way).start()

    launch(order[0], 0)
    for i, slot in enumerate(order):
        if i + 1 < cap:
            launch(order[i + 1], 0)
        place(slot, z)[...] = steps_ref[slot]
        for s in range(nz - 1):
            for way in (1, -1):

                @pl.when(receives(s, way))
                def _():
                    arrival(slot, s, way).wait_recv()

                if s + 1 < nz - 1:

                    @pl.when(sends(s + 1, way))
                    def _():
                        hop(slot, s + 1, way).start()

        if slot > 0:
            @pl.when(t == nt - 1)
            def _():
                def early(k, _):
                    days(k * pair, pair, carry, out_ref, [slot])
                    return 0

                lax.fori_loop(0, chunks // pair, early, 0)

    def pass_on(k, device):
        return pltpu.make_async_remote_copy(
            src_ref=out_ref.at[0, :, stripe(k)],
            dst_ref=carry.at[:, stripe(k)],
            send_sem=csend.at[k],
            recv_sem=crecv.at[k],
            device_id={"tm": device},
            device_id_type=MESH,
        )

    def scout_on(k, device):
        return pltpu.make_async_remote_copy(
            src_ref=scout_out.at[0, :, stripe(k)],
            dst_ref=scout_in.at[:, stripe(k)],
            send_sem=ssend.at[k],
            recv_sem=srecv.at[k],
            device_id={"tm": device},
            device_id_type=MESH,
        )

    def hand_over(k):
        return pltpu.make_async_remote_copy(
            src_ref=scout_out.at[0, :, stripe(k)],
            dst_ref=carry.at[:, stripe(k)],
            send_sem=hsend.at[k],
            recv_sem=crecv.at[k],
            device_id={"tm": t - 1, "space": end},
            device_id_type=MESH,
        )

    @pl.when(scouts & (t >= span))
    def _():
        def scout_chunk(k, _):
            scout_on(k, t - 1).wait_recv()
            days(k, 1, scout_in, scout_out, order)

            @pl.when(edge)
            def _():
                hand_over(k).start()

            @pl.when(t > span)
            def _():
                scout_on(k, t - 1).start()

            return 0

        lax.fori_loop(0, chunks, scout_chunk, 0)

    passes = (t > 0) & jnp.logical_not(at_end & edge)

    def chain(count):
        def one_chunk(j, _):
            @pl.when(t < nt - 1)
            def _():
                for k in range(count):
                    pass_on(j * count + k, t + 1).wait_recv()
                days(j * count, count, carry, out_ref, order)

            @pl.when(t == nt - 1)
            def _():
                days(j * count, count, carry, out_ref, order[-1:])

            @pl.when(passes)
            def _():
                for k in range(count):
                    pass_on(j * count + k, t - 1).start()

            return 0

        lax.fori_loop(0, chunks // count, one_chunk, 0)

    @pl.when(at_end)
    def _():
        chain(pair)

    @pl.when(jnp.logical_not(at_end))
    def _():
        chain(1)

    @pl.when(lends)
    def _():
        for k in range(chunks):
            lend(k, scout).wait_send()

    @pl.when(scouts & (t > span))
    def _():
        for k in range(chunks):
            scout_on(k, t - 1).wait_send()

    @pl.when(gives)
    def _():
        for k in range(chunks):
            hand_over(k).wait_send()

    for slot in order:
        for s in range(nz - 1):
            for way in (1, -1):

                @pl.when(sends(s, way))
                def _():
                    hop(slot, s, way).wait_send()

    @pl.when(passes)
    def _():
        for k in range(chunks):
            pass_on(k, t - 1).wait_send()


def shards(nt, nz, steps, lengths, anchor):
    cap, rows, nodes = steps.shape
    width = anchor.shape[1]
    chunks = width // min(CHUNK, width)
    vmem = pl.BlockSpec(memory_space=pltpu.VMEM)
    panels = pl.pallas_call(
        functools.partial(kernel, nt, nz),
        out_shape=jax.ShapeDtypeStruct((cap, nodes, width), jnp.bfloat16),
        in_specs=[pl.BlockSpec(memory_space=pltpu.SMEM), vmem, vmem],
        out_specs=vmem,
        scratch_shapes=[
            pltpu.VMEM((cap, nodes, nodes), jnp.bfloat16),
            pltpu.VMEM((nodes, width), jnp.bfloat16),
            pltpu.VMEM((cap, nodes, width), jnp.bfloat16),
            pltpu.VMEM((nodes, width), jnp.bfloat16),
            pltpu.SemaphoreType.DMA((2, cap, nz - 1)),
            pltpu.SemaphoreType.DMA((2, cap, nz - 1)),
            pltpu.SemaphoreType.DMA((chunks,)),
            pltpu.SemaphoreType.DMA((chunks,)),
            pltpu.SemaphoreType.DMA((chunks,)),
            pltpu.SemaphoreType.DMA((chunks,)),
            pltpu.SemaphoreType.DMA((chunks,)),
            pltpu.SemaphoreType.DMA((chunks,)),
        ],
        compiler_params=pltpu.CompilerParams(
            collective_id=0, has_side_effects=True, vmem_limit_bytes=GRANT
        ),
    )(lengths, steps, anchor)
    used = jnp.arange(cap) < lengths[0]
    return jnp.where(used[:, None, None], panels.astype(jnp.float32), 0.0)


def solution(mesh):
    return jax.shard_map(
        functools.partial(shards, mesh.shape["tm"], mesh.shape["space"]),
        mesh=mesh,
        in_specs=(P("tm", "space", None), P("tm"), P(None, "space")),
        out_specs=P("tm", None, "space"),
        check_vma=False,
    )
```
